32 devices in a mesh: groups: 2 (over y), dp: 8 (over z, x), section: 2 (over core).
Axes of the slice: x: 2, y: 2, z: 4, core: 2. Of those that a mesh axis runs over, the one named last changes fastest.
Arguments:
- latents: bfloat16 [2048, 3072], P(('groups', 'dp')), parts along dimension 0, may hold values from -6 to 6
- out_grad: float32 [2048, 3072], P(('groups', 'dp')), parts along dimension 0, may hold values from -0.3 to 0.3
- frozen_weight: bfloat16 [2, 3072, 1536], P('section', 'dp'), may hold values from -0.109375 to 0.109375
- norm_gain: float32 [2, 3072], P('section'), may hold values from 0.5 to 1.5
- time_gate: float32 [2, 50], P('section'), may hold values from 0.5 to 2
- down_factors: bfloat16 [2, 96, 64, 3072], P('section', ('groups', 'dp')), parts along dimension 1, may hold values from -0.109375 to 0.109375
- up_factors: bfloat16 [2, 96, 64, 1536], P('section', ('groups', 'dp')), parts along dimension 1, may hold values from -0.75 to 0.75
- block_jobs: int32 [16], P('groups'), parts along dimension 0, may hold values from 0 to 47
- owners: int32 [96], P('groups'), parts along dimension 0, may hold values from 0 to 47, as said below
- block_steps: int32 [16], P(('groups', 'dp')), parts along dimension 0, may hold values from 0 to 49
- block_fill: int32 [16], P(('groups', 'dp')), parts along dimension 0, may hold values from 1 to 128, as said below
Outputs:
- grad_down: float32 [2, 96, 64, 3072], P('section', ('groups', 'dp')), parts along dimension 1
- grad_up: float32 [2, 96, 64, 1536], P('section', ('groups', 'dp')), parts along dimension 1
The draws below stay inside these ranges and needn't reach their ends.
There are 2 independent parts, one for each index of `groups`. The reference program is written for one: setup_inputs(seed, part) draws one part's arguments, and reference() takes and returns one part's arrays. A program takes and returns all parts, laid end to end along the dimension named above; an argument that names none is the same for every part. Nothing has to cross between parts.
Inputs may be any that keep to these rules, and one draw needn't show every extreme that they name: `owners`: no two adapters share a slot; slot 0 and the last slot always hold one. `block_fill`: the live rows come first in their block; in every draw some block is full and some holds a single live row.
All inputs are finite; a program needn't handle non-finite values.
Results may differ from the reference program's by a relative error of at most 0.006.
Values may be sent and summed in bfloat16 or wider, within the bound.
No kernel may reach another device: no remote copies, remote signals or barrier semaphores. Data moves between devices by JAX's collectives and lax.ppermute only.
A program may use at most 128 MiB of HBM per device.

```python
import math
import jax
import jax.numpy as jnp
import numpy as np
from jax import lax

D = 3072
H = 1536
R = 64
ADAPTERS = 48
TSTEPS = 50
BLK = 128
SLOT_COUNT = 48
BLOCKS = 8
ROWS = 1024


def draw_owners(key, part):
    middle = jax.random.permutation(jax.random.fold_in(key, 11), SLOT_COUNT - 2).astype(jnp.int32) + 1
    picked = jnp.concatenate([jnp.zeros((1,), jnp.int32), middle[:ADAPTERS - 2], jnp.full((1,), SLOT_COUNT - 1, jnp.int32)])
    return jax.random.permutation(jax.random.fold_in(key, 12), picked).astype(jnp.int32)


def draw_block_fill(key, part):
    counts = jax.random.randint(jax.random.fold_in(key, 21), (BLOCKS,), 1, BLK + 1).astype(jnp.int32)
    full_at = jax.random.randint(jax.random.fold_in(key, 22), (), 0, BLOCKS).astype(jnp.int32)
    counts = counts.at[full_at].set(BLK)
    counts = counts.at[(full_at + 1) % BLOCKS].set(1)
    return counts.astype(jnp.int32)


def set_ends(array, rng, least, high):
    longest = array.shape.index(max(array.shape))
    spots = []
    for shift in (0, 1):
        where = [jax.random.randint(jax.random.fold_in(rng, axis), (), 0, length) for axis, length in enumerate(array.shape)]
        where[longest] = (where[longest] + shift) % array.shape[longest]
        spots.append(tuple(where))
    return array.at[spots[0]].set(least).at[spots[1]].set(high)


def level_of(stream_key, extent, cuts, smallest, high):
    gain, own = 1.0, jax.random.fold_in(stream_key, 6)
    for position, blocks in cuts:
        draws = jnp.exp(jax.random.uniform(jax.random.fold_in(own, position), (blocks,), jnp.float32, smallest / len(cuts), high / len(cuts)))
        gain = gain * jnp.repeat(draws, extent[position] // blocks).reshape([-1 if axis == position else 1 for axis in range(len(extent))])
    return gain


def cumulative_ranks(amount, lean):
    weights = [(1 << 20) // math.isqrt(standing ** lean) + 1 for standing in range(1, amount + 1)]
    spread = 1 + sum(weights) // (1 << 30)
    return np.cumsum(np.array([max(1, weight // spread) for weight in weights]))


def skewed_ids(stream_key, shape, count, skew):
    listing = cumulative_ranks(count, skew)
    ticket = jax.random.randint(jax.random.fold_in(stream_key, 1), shape, 0, int(listing[count - 1]))
    rank = jnp.searchsorted(jnp.asarray(listing, jnp.int32), ticket, side="right")
    return jax.random.permutation(jax.random.fold_in(stream_key, 2), count)[rank].astype(jnp.int32)


def scatter_about(rng, shape, spread, most, cuts=(), held_as=jnp.bfloat16):
    result = spread * jax.random.normal(rng, shape, jnp.float32)
    if cuts:
        result = result * level_of(rng, shape, cuts, -0.22, 0.18)
    return jnp.clip(result, -most, most).astype(held_as)


def setup_inputs(seed: int = 0, part: int = 0) -> dict:
    key_list = jax.random.split(jax.random.key(seed), 12)
    own_keys = jax.random.split(jax.random.fold_in(key_list[11], part), 12)
    return {
        "latents": scatter_about(own_keys[0], (ROWS, D), 1.0, 6.0, ((0, 8),)),
        "out_grad": scatter_about(own_keys[1], (ROWS, D), 0.05, 0.3, ((0, 8),), jnp.float32),
        "frozen_weight": scatter_about(key_list[2], (2, D, H), D ** -0.5, 0.109375, ((0, 2), (1, 8))),
        "norm_gain": jnp.clip(1.0 + 0.1 * jax.random.normal(key_list[3], (2, D), jnp.float32), 0.5, 1.5),
        "time_gate": jnp.clip(jnp.exp(math.log(2.0) - 1.3862944 * jax.random.uniform(key_list[4], (2, TSTEPS), jnp.float32) ** level_of(key_list[4], (2, TSTEPS), ((0, 2),), -0.2, 0.2)), 0.5, 2.0),
        "down_factors": scatter_about(own_keys[5], (2, SLOT_COUNT, R, D), D ** -0.5, 0.109375, ((0, 2), (1, 8))),
        "up_factors": scatter_about(own_keys[6], (2, SLOT_COUNT, R, H), R ** -0.5, 0.75, ((0, 2), (1, 8))),
        "block_jobs": set_ends(skewed_ids(own_keys[7], (BLOCKS,), ADAPTERS, 2), jax.random.fold_in(own_keys[7], 3), 0, ADAPTERS - 1).astype(jnp.int32),
        "owners": draw_owners(jax.random.fold_in(jax.random.fold_in(key_list[11], part), 71), part),
        "block_steps": set_ends(jax.random.randint(own_keys[9], (BLOCKS,), 0, TSTEPS), jax.random.fold_in(own_keys[9], 1), 0, TSTEPS - 1).astype(jnp.int32),
        "block_fill": draw_block_fill(jax.random.fold_in(jax.random.fold_in(key_list[11], part), 71), part),
    }


epsilon = 1e-06

def matrix_product(spec, left_op, right_op):
    return jnp.einsum(spec, left_op.astype(jnp.float32), right_op.astype(jnp.float32), precision=lax.Precision.HIGHEST)

def forward_pass(inputs, frozen_layer, gain_row, down_projection_block, up_block, scales):
    out_width = up_block.shape[2]
    values = inputs.astype(jnp.float32)
    inverse = lax.rsqrt(lax.optimization_barrier(jnp.mean(values * values, axis=2)) + epsilon)
    normalized_input = (values * inverse[:, :, None] * gain_row).astype(jnp.bfloat16)
    frozen_out = matrix_product('bmd,dh->bmh', normalized_input, frozen_layer)
    reduced_features = matrix_product('uyi,uoi->uyo', normalized_input, down_projection_block).astype(jnp.bfloat16)
    extra = matrix_product('bmq,bqh->bmh', reduced_features, up_block)
    update = scales[:, None, None] * (frozen_out + extra)
    window_out = (values[:, :, :out_width] + update).astype(jnp.bfloat16)
    outputs = jnp.concatenate([window_out, inputs[:, :, out_width:]], axis=2)
    return (outputs, normalized_input, inverse, reduced_features)

def backward_pass(inputs, normalized_input, inverse, reduced_features, cotangent, frozen_layer, gain_row, down_projection_block, up_block, scales):
    out_width = up_block.shape[2]
    values = inputs.astype(jnp.float32)
    delta_output = (scales[:, None, None] * cotangent[:, :, :out_width]).astype(jnp.bfloat16)
    grad_upper = matrix_product('bmq,bmh->bqh', reduced_features, delta_output)
    low_rank_delta = matrix_product('bmh,bqh->bmq', delta_output, up_block).astype(jnp.bfloat16)
    lower_gradient = matrix_product('hoc,hou->hcu', low_rank_delta, normalized_input)
    delta_normalized = matrix_product('way,cy->wac', delta_output, frozen_layer) + matrix_product('rha,rak->rhk', low_rank_delta, down_projection_block)
    scaled = gain_row * delta_normalized
    inner = lax.optimization_barrier(jnp.mean(values * scaled, axis=2))
    cubed = inverse * inverse * inverse
    delta_in = inverse[:, :, None] * scaled - values * (cubed * inner)[:, :, None]
    carried = (cotangent + delta_in).astype(jnp.bfloat16)
    return (carried, lower_gradient, grad_upper)

def reference(latents, out_grad, frozen_weight, norm_gain, time_gate, down_factors, up_factors, block_jobs, owners, block_steps, block_fill):
    slot_of = owners[block_jobs].astype(jnp.int32)
    inputs = latents.reshape(BLOCKS, BLK, D)
    live_rows = jnp.arange(BLK, dtype=jnp.int32)[None, :] < block_fill[:, None]
    cotangent = jnp.where(live_rows[:, :, None], out_grad.reshape(BLOCKS, BLK, D), 0.0)
    stored = []
    for layer_index in range(2):
        down_projection_block = down_factors[layer_index][slot_of]
        up_block = up_factors[layer_index][slot_of]
        scales = time_gate[layer_index][block_steps]
        outputs, normalized_input, inverse, reduced_features = forward_pass(inputs, frozen_weight[layer_index], norm_gain[layer_index], down_projection_block, up_block, scales)
        stored.append((inputs, normalized_input, inverse, reduced_features, down_projection_block, up_block, scales))
        inputs = outputs
    results = []
    for layer_index in (1, 0):
        saved_in, normalized_input, inverse, reduced_features, down_projection_block, up_block, scales = stored[layer_index]
        carried, lower_gradient, grad_upper = backward_pass(saved_in, normalized_input, inverse, reduced_features, cotangent, frozen_weight[layer_index], norm_gain[layer_index], down_projection_block, up_block, scales)
        cotangent = carried.astype(jnp.float32)
        summed_down = jax.ops.segment_sum(lower_gradient, slot_of, num_segments=SLOT_COUNT)
        summed_up = jax.ops.segment_sum(grad_upper, slot_of, num_segments=SLOT_COUNT)
        results.append((summed_down, summed_up))
    grad_down = jnp.stack([results[1][0], results[0][0]])
    grad_up = jnp.stack([results[1][1], results[0][1]])
    return (grad_down, grad_up)
```

```python
import jax
import jax.numpy as jnp
from jax import lax
from jax.experimental import pallas as pl
from jax.experimental.pallas import tpu as pltpu
from jax.sharding import PartitionSpec as P

epsilon = 1e-06


def passed_along(value, axis, steps):
    count = lax.axis_size(axis)
    leading, last = (max(0, -steps), min(count, count - steps))
    return lax.ppermute(value, axis, [(source, source + steps) for source in range(leading, last)])


def matrix_product(spec, left_op, right_op):
    return jnp.einsum(spec, left_op, right_op, preferred_element_type=jnp.float32)


def forward_pass(inputs, frozen_layer, gain_row, down_projection_block, up_block, scales):
    out_width = up_block.shape[2]
    block_total, row_count, model_width = inputs.shape
    values = inputs.astype(jnp.float32)
    inverse = lax.rsqrt(jnp.mean(values * values, axis=2) + epsilon)
    normalized_input = (values * inverse[:, :, None] * gain_row).astype(jnp.bfloat16)
    frozen_out = jnp.dot(
        normalized_input.reshape(block_total * row_count, model_width),
        frozen_layer,
        preferred_element_type=jnp.float32,
    )
    frozen_out = frozen_out.reshape(block_total, row_count, out_width)
    reduced_features = matrix_product(
        "uyi,uoi->uyo", normalized_input, down_projection_block
    ).astype(jnp.bfloat16)
    extra = matrix_product("bmq,bqh->bmh", reduced_features, up_block)
    update = scales[:, None, None] * (frozen_out + extra)
    window_out = (values[:, :, :out_width] + update).astype(jnp.bfloat16)
    outputs = jnp.concatenate([window_out, inputs[:, :, out_width:]], axis=2)
    return (outputs, (inputs, normalized_input, inverse, reduced_features))


def backward_pass(
    stored, cotangent, frozen_layer, gain_row, down_projection_block, up_block, scales
):
    inputs, normalized_input, inverse, reduced_features = stored
    out_width = up_block.shape[2]
    block_total, row_count, model_width = inputs.shape
    values = inputs.astype(jnp.float32)
    delta_output = (scales[:, None, None] * cotangent[:, :, :out_width]).astype(jnp.bfloat16)
    grad_upper = matrix_product("bmq,bmh->bqh", reduced_features, delta_output)
    low_rank_delta = matrix_product("bmh,bqh->bmq", delta_output, up_block).astype(jnp.bfloat16)
    lower_gradient = matrix_product("hoc,hou->hcu", low_rank_delta, normalized_input)
    through = lax.dot_general(
        delta_output.reshape(block_total * row_count, out_width),
        frozen_layer,
        (((1,), (1,)), ((), ())),
        preferred_element_type=jnp.float32,
    )
    delta_normalized = through.reshape(block_total, row_count, model_width) + matrix_product(
        "rha,rak->rhk", low_rank_delta, down_projection_block
    )
    scaled = gain_row * delta_normalized
    inner = jnp.mean(values * scaled, axis=2)
    cubed = inverse * inverse * inverse
    delta_in = inverse[:, :, None] * scaled - values * (cubed * inner)[:, :, None]
    carried = (cotangent + delta_in).astype(jnp.bfloat16)
    return (carried, lower_gradient, grad_upper)


def spread_body(
    latents,
    out_grad,
    frozen_weight,
    norm_gain,
    time_gate,
    down_factors,
    up_factors,
    block_jobs,
    owners,
    block_steps,
    block_fill,
):
    position = lax.axis_index("section")
    lane_count = lax.axis_size("dp")
    slot_local = down_factors.shape[1]
    low_rank = down_factors.shape[2]
    model_width = down_factors.shape[3]
    blocks_dev = block_fill.shape[0]
    block_rows = latents.shape[0] // blocks_dev
    is_first = position == 0
    frozen_layer = lax.all_gather(frozen_weight[0], "dp", axis=0, tiled=True)
    gain_row = norm_gain[0]
    gate_row = time_gate[0]
    chosen = block_steps[:, None] == jnp.arange(gate_row.shape[0], dtype=jnp.int32)[None, :]
    scales = jnp.sum(jnp.where(chosen, gate_row[None, :], 0.0), axis=1)
    matches = block_jobs[:, None] == jnp.arange(owners.shape[0], dtype=jnp.int32)[None, :]
    slot_of = jnp.sum(jnp.where(matches, owners[None, :], 0), axis=1)
    spread_down, spread_up = (
        lax.all_to_all(down_factors[0], "dp", split_axis=2, concat_axis=0, tiled=True),
        lax.all_to_all(up_factors[0], "dp", split_axis=2, concat_axis=0, tiled=True),
    )
    down_projection_block, up_block = (
        lax.all_to_all(spread_down[slot_of], "dp", split_axis=0, concat_axis=2, tiled=True),
        lax.all_to_all(spread_up[slot_of], "dp", split_axis=0, concat_axis=2, tiled=True),
    )
    micro_count = 1
    micro_rows = block_rows // micro_count
    block_view = latents.reshape(blocks_dev, block_rows, model_width)
    live_rows = jnp.arange(block_rows, dtype=jnp.int32)[None, :] < block_fill[:, None]
    masked = jnp.where(
        live_rows[:, :, None], out_grad.reshape(blocks_dev, block_rows, model_width), 0.0
    )
    incoming = jnp.zeros((blocks_dev, micro_rows, model_width), jnp.bfloat16)
    kept = []
    for turn_index in range(micro_count + 1):
        source = jnp.where(is_first, block_view, incoming)
        outputs, stored = forward_pass(
            source, frozen_layer, gain_row, down_projection_block, up_block, scales
        )
        kept.append(stored)
        if turn_index < micro_count:
            incoming = passed_along(outputs, "section", 1)
    states = [
        jax.tree.map(lambda former, latter: jnp.where(is_first, former, latter), kept[0], kept[1])
    ]
    returned = jnp.zeros((blocks_dev, micro_rows, model_width), jnp.bfloat16)
    sum_down = jnp.zeros((blocks_dev, low_rank, model_width), jnp.float32)
    sum_up = jnp.zeros((blocks_dev, low_rank, up_block.shape[2]), jnp.float32)
    for turn_index in range(micro_count + 1):
        late_micro = min(turn_index, micro_count - 1)
        early_micro = max(turn_index - 1, 0)
        current = jax.tree.map(
            lambda former, latter: jnp.where(is_first, former, latter),
            states[early_micro],
            states[late_micro],
        )
        cotangent = jnp.where(is_first, returned.astype(jnp.float32), masked)
        carried, lower_gradient, grad_upper = backward_pass(
            current, cotangent, frozen_layer, gain_row, down_projection_block, up_block, scales
        )
        useful = jnp.where(is_first, turn_index >= 1, turn_index < micro_count)
        sum_down = sum_down + jnp.where(useful, lower_gradient, 0.0)
        sum_up = sum_up + jnp.where(useful, grad_upper, 0.0)
        if turn_index < micro_count:
            returned = passed_along(carried, "section", -1)
    pieces_down, pieces_up = (
        lax.all_to_all(sum_down, "dp", split_axis=2, concat_axis=0, tiled=True),
        lax.all_to_all(sum_up, "dp", split_axis=2, concat_axis=0, tiled=True),
    )
    slot_total = lane_count * slot_local
    onehot = (jnp.arange(slot_total, dtype=jnp.int32)[:, None] == slot_of[None, :]).astype(
        jnp.float32
    )
    block_total = pieces_down.shape[0]
    slot_down = jnp.dot(
        onehot,
        pieces_down.reshape(block_total, -1),
        precision=lax.Precision.HIGHEST,
        preferred_element_type=jnp.float32,
    )
    slot_up = jnp.dot(
        onehot,
        pieces_up.reshape(block_total, -1),
        precision=lax.Precision.HIGHEST,
        preferred_element_type=jnp.float32,
    )
    slot_down = slot_down.reshape(slot_total, low_rank, pieces_down.shape[2])
    slot_up = slot_up.reshape(slot_total, low_rank, pieces_up.shape[2])
    owned_down, owned_up = (
        lax.all_to_all(slot_down, "dp", split_axis=0, concat_axis=2, tiled=True),
        lax.all_to_all(slot_up, "dp", split_axis=0, concat_axis=2, tiled=True),
    )
    return (owned_down[None], owned_up[None])


def swapped(value):
    return lax.ppermute(value, "section", [(0, 1), (1, 0)])


def ring_place(index, count):
    return jnp.where(index % 2 == 0, index // 2, count - 1 - index // 2)


def ring_member(place, count):
    place = place % count
    return jnp.where(place < count // 2, 2 * place, 2 * (count - 1 - place) + 1)


def ring_pairs(groups, count, sign):
    order = [*range(0, count, 2), *range(count - 1, 0, -2)]
    pairs = []
    for group in range(groups):
        for place in range(count):
            for core in range(2):
                step = sign if core == 0 else -sign
                source = (group * count + order[place]) * 2 + core
                target = (group * count + order[(place + step) % count]) * 2 + core
                pairs.append((source, target))
    return pairs


LANES = 128
CHUNK = 16


def product(left, right, contract):
    dims = ((contract[:1], contract[1:]), ((), ()))
    return lax.dot_general(left, right, dims, preferred_element_type=jnp.float32)


def slot_columns(slot, rank, columns):
    column = lax.broadcasted_iota(jnp.int32, (1, columns), 1)
    return (column >= slot * rank) & (column < (slot + 1) * rank)


def whole(memory_space=pltpu.VMEM):
    return pl.BlockSpec(memory_space=memory_space)


def call(kernel, outs, args, spaces, scratch=(), flops=0, out_spaces=None):
    moved = sum(a.size * a.dtype.itemsize for a in (*args, *outs))
    single = not isinstance(outs, (tuple, list))
    return pl.pallas_call(
        kernel,
        out_shape=outs,
        in_specs=[whole(space) for space in spaces],
        out_specs=[whole(out_spaces[i] if out_spaces else pltpu.VMEM) for i in range(len(outs))],
        scratch_shapes=list(scratch),
        cost_estimate=pl.CostEstimate(flops=flops, bytes_accessed=moved, transcendentals=0),
    )(*args)


def shaped(dtype, *shape):
    return jax.ShapeDtypeStruct(shape, dtype)


def contribution_kernel(sizes, rank, *refs):
    count = len(sizes)
    scalars = refs[0]
    lats, deltas = refs[1 : 1 + count], refs[1 + count : 1 + 2 * count]
    gain_0, gain_1 = refs[1 + 2 * count : 3 + 2 * count]
    sources = refs[3 + 2 * count : 9 + 2 * count]
    update, head, inner, keep, give = refs[9 + 2 * count : 14 + 2 * count]
    normed, tail, delta, slice_1, *held, sems = refs[14 + 2 * count :]
    f32, bf16 = jnp.float32, jnp.bfloat16
    core, offset = scalars[0], pl.multiple_of(scalars[1], LANES)
    out_width = update.shape[1]
    width = normed.shape[1]
    own_columns = slice_1.shape[1]
    columns = held[0].shape[0]
    total = sum(sizes)

    def copies(swap):
        order = [sources[(i + 3) % 6] for i in range(6)] if swap else sources
        return [pltpu.make_async_copy(order[i], held[i], sems.at[i]) for i in range(6)]

    @pl.when(core == 0)
    def _():
        for copy in copies(False):
            copy.start()

    @pl.when(core != 0)
    def _():
        for copy in copies(True):
            copy.start()

    waits = copies(False)
    begin = 0
    for index, size in enumerate(sizes):
        lat, grad = lats[index], deltas[index]
        from_row = core * size if lat.shape[0] != size else 0

        def rows_step(step, carry, lat=lat, grad=grad, from_row=from_row, begin=begin):
            source = pl.ds(pl.multiple_of(from_row + step * CHUNK, CHUNK), CHUNK)
            target = pl.ds(pl.multiple_of(begin + step * CHUNK, CHUNK), CHUNK)
            values = lat[source, :].astype(f32)
            inverse = lax.rsqrt(jnp.mean(values * values, axis=1, keepdims=True) + epsilon)
            normed[target, :] = (values * inverse * gain_0[...]).astype(bf16)
            tail[target, :] = (values[:, out_width:] * gain_1[:, out_width:]).astype(bf16)
            delta[target, :] = grad[source, :]
            slice_1[target, :] = lat[source, pl.ds(offset, own_columns)].astype(f32) * gain_1[
                :, pl.ds(offset, own_columns)
            ]
            far = jnp.where(core == 0, 1, 0)

            @pl.when(core == 0)
            def _():
                give[target, : width - out_width] = lat[source, out_width:]

            @pl.when(core != 0)
            def _():
                keep[target, : width - out_width] = lat[source, out_width:]

            return carry

        lax.fori_loop(0, size // CHUNK, rows_step, 0)
        begin += size

    row = lax.broadcasted_iota(jnp.int32, (total, 1), 0)
    slot = jnp.zeros((total, 1), jnp.int32) + scalars[2]
    begin = sizes[0]
    for index in range(1, count):
        slot = jnp.where(row >= begin, scalars[2 + index], slot)
        begin += sizes[index]
    column = lax.broadcasted_iota(jnp.int32, (total, columns), 1)
    mask = (column >= slot * rank) & (column < (slot + 1) * rank)

    down_0, up_0, frozen_0, down_1, up_1, frozen_1 = held
    waits[0].wait()
    low = jnp.where(mask, product(normed[...], down_0[...], (1, 1)), 0.0).astype(bf16)
    waits[1].wait()
    waits[2].wait()
    update[...] = (
        product(normed[:, pl.ds(offset, own_columns)], frozen_0[...], (1, 0))
        + product(low, up_0[...], (1, 0))
    ).astype(update.dtype)
    waits[4].wait()
    low_grad = jnp.where(mask, product(delta[...], up_1[...], (1, 1)), 0.0).astype(bf16)
    waits[5].wait()
    slab = product(delta[...], frozen_1[...], (1, 1))
    waits[3].wait()
    head[...] = product(low_grad, down_1[:, :out_width], (1, 0))
    tail_low = product(tail[...], down_1[:, out_width:], (1, 1))
    inner_low = jnp.sum(low_grad.astype(f32) * tail_low, axis=1, keepdims=True)

    @pl.when(offset < out_width)
    def _():
        head[:, pl.ds(offset, own_columns)] += slab
        inner[...] = jnp.broadcast_to(inner_low, inner.shape)

    @pl.when(offset >= out_width)
    def _():
        own = inner_low + jnp.sum(slice_1[...] * slab, axis=1, keepdims=True)
        inner[...] = jnp.broadcast_to(own, inner.shape)

    def fill(zeroth, oneth):
        zeroth[:, :width] = normed[...]
        zeroth[:, width:] = low
        oneth[:, width - out_width : width] = delta[...]
        oneth[:, width:] = low_grad

    @pl.when(core == 0)
    def _():
        fill(keep, give)

    @pl.when(core != 0)
    def _():
        fill(give, keep)


def contribution(scalars, segments, gains, sources, slots, rank, out_width):
    f32, bf16 = jnp.float32, jnp.bfloat16
    sizes = tuple(size for _, _, size in segments)
    total = sum(sizes)
    columns, width = sources[0].shape
    own_columns = sources[2].shape[0]
    args = [scalars, *(s[0] for s in segments), *(s[1] for s in segments), *gains, *sources]
    spaces = [pltpu.SMEM] + [pltpu.VMEM] * (2 * len(sizes) + 2) + [pl.ANY] * 6
    outs = [
        shaped(f32, total, out_width),
        shaped(f32, total, out_width),
        shaped(f32, total, LANES),
        shaped(bf16, total, width + columns),
        shaped(bf16, total, width + columns),
    ]
    scratch = [
        pltpu.VMEM((total, width), bf16),
        pltpu.VMEM((total, width - out_width), bf16),
        pltpu.VMEM((total, out_width), bf16),
        pltpu.VMEM((total, own_columns), f32),
        *(pltpu.VMEM(sources[i % 3].shape, bf16) for i in range(6)),
        pltpu.SemaphoreType.DMA((6,)),
    ]
    flops = 2 * total * columns * (2 * width + 3 * out_width) * 2
    return call(
        lambda *refs: contribution_kernel(sizes, rank, *refs), outs, args, spaces, scratch, flops
    )


def packed_inner(inner):
    lane = lax.broadcasted_iota(jnp.int32, inner.shape, 1)
    high = inner.astype(jnp.bfloat16)
    low = (inner - high.astype(jnp.float32)).astype(jnp.bfloat16)
    zero = jnp.zeros_like(high)
    return jnp.where(lane == 0, high.astype(jnp.float32), jnp.where(lane == 1, low.astype(jnp.float32), 0.0)).astype(jnp.bfloat16)


def unpacked_inner(value):
    return jnp.sum(value.astype(jnp.float32), axis=1, keepdims=True)


def chained(scalars, received, own, start, size, inner=None):
    f32, bf16 = jnp.float32, jnp.bfloat16
    got = received.shape[0] if received is not None else 0
    rows = max(got, size)
    out_width = own.shape[1]
    extra = 0 if inner is None else LANES

    def kernel(scalars, *refs):
        refs = list(refs)
        arrived = refs.pop(0) if got else None
        own, inner = refs[0], (refs[1] if extra else None)
        out = refs[-1]
        core = scalars[0]

        def step(index, carry):
            base = index * CHUNK
            target = pl.ds(pl.multiple_of(base, CHUNK), CHUNK)

            def gather(wide, narrow):
                total = wide
                return total

            low = core * (rows // 2)
            inside = (base >= low) & (base < low + rows // 2)
            local = jnp.where(inside, base - low, 0)
            if got == 0:
                main, extra_rows = own[pl.ds(pl.multiple_of(start + base, CHUNK), CHUNK), :], None
                scalar = inner[pl.ds(pl.multiple_of(start + base, CHUNK), CHUNK), :] if extra else None
            else:
                full = got == rows and size == rows
                at_got = base if got == rows else local
                at_own = start + (base if size == rows else local)
                theirs = arrived[pl.ds(pl.multiple_of(at_got, CHUNK), CHUNK), :].astype(f32)
                ours = own[pl.ds(pl.multiple_of(at_own, CHUNK), CHUNK), :]
                if extra:
                    inner_ours = inner[pl.ds(pl.multiple_of(at_own, CHUNK), CHUNK), :]
                    inner_theirs = jnp.sum(theirs[:, out_width:], axis=1, keepdims=True)
                    theirs = theirs[:, :out_width]
                if got != rows:
                    theirs = jnp.where(inside, theirs, 0.0)
                    if extra:
                        inner_theirs = jnp.where(inside, inner_theirs, 0.0)
                if size != rows:
                    ours = jnp.where(inside, ours, 0.0)
                    if extra:
                        inner_ours = jnp.where(inside, inner_ours, 0.0)
                main = theirs + ours
                scalar = inner_theirs + inner_ours if extra else None
            out[target, :out_width] = main.astype(bf16)
            if extra:
                out[target, out_width:] = packed_inner(scalar)
            return carry

        lax.fori_loop(0, rows // CHUNK, step, 0)

    args = [scalars, *([received] if got else []), own, *([inner] if extra else [])]
    spaces = [pltpu.SMEM] + [pltpu.VMEM] * (len(args) - 1)
    return call(kernel, [shaped(bf16, rows, out_width + extra)], args, spaces)[0]


def owner_kernel(scalars, scales, update_a, update_b, head_a, head_b, lat, grad, gain_1, head_next, delta_0):
    f32, bf16 = jnp.float32, jnp.bfloat16
    rows, out_width = head_next.shape
    width = lat.shape[1]
    scale_0, fill = scales[0], scalars[1]

    def step(index, carry):
        at = pl.ds(pl.multiple_of(index * CHUNK, CHUNK), CHUNK)
        values = lat[at, :].astype(f32)
        update = update_a[at, :].astype(f32) + update_b[at, :].astype(f32)
        new = (values[:, :out_width] + scale_0 * update).astype(bf16)
        head_next[at, :] = new
        new = new.astype(f32)
        tail = values[:, out_width:]
        total = jnp.sum(new * new, axis=1, keepdims=True) + jnp.sum(tail * tail, axis=1, keepdims=True)
        inverse = lax.rsqrt(total / width + epsilon)
        slope = head_a[at, :].astype(f32) + head_b[at, :].astype(f32)
        scaled = gain_1[:, :out_width] * slope[:, :out_width]
        inner = jnp.sum(new * scaled, axis=1, keepdims=True) + jnp.sum(slope[:, out_width:], axis=1, keepdims=True)
        cubed = inverse * inverse * inverse
        row = lax.broadcasted_iota(jnp.int32, (CHUNK, 1), 0) + index * CHUNK
        top = jnp.where(row < fill, grad[at, :], 0.0)
        carried = (top + (inverse * scaled - new * (cubed * (inner / width)))).astype(bf16)
        delta_0[at, :] = (scale_0 * carried.astype(f32)).astype(bf16)
        return carry

    lax.fori_loop(0, rows // CHUNK, step, 0)


def gradient_kernel(sizes, rank, *refs):
    f32, bf16 = jnp.float32, jnp.bfloat16
    batches = len(sizes)
    hops = batches
    take = iter(refs)
    scalars, gain_1 = next(take), next(take)
    keeps = [next(take) for _ in range(batches)]
    gots = [next(take) for _ in range(batches)]
    head_own, delta_own = next(take), next(take)
    heads = [next(take) for _ in range(hops)]
    deltas = [next(take) for _ in range(hops)]
    lates = [next(take) for _ in range(hops)]
    down, up = next(take), next(take)
    grad_down, grad_up = next(take), next(take)
    normed, low_grad, low, delta, head, out_down, out_up, sems, out_sems = take
    core = scalars[0]
    rows, width = normed.shape
    out_width = delta.shape[1]
    half = head_own.shape[0] // 2
    tail_width = width - out_width
    piece = [half, *(each.shape[0] for each in heads)]
    block_slots = [scalars[2 + i] for i in range(2 * len(piece))]

    def batch_copies(first_layer):
        copies = []
        begin = 0
        for side in (keeps, gots):
            for source in side:
                size = source.shape[0]
                at = pl.ds(begin, size)
                if first_layer:
                    parts = [(source.at[:, pl.ds(0, width)], normed.at[at]), (source.at[:, pl.ds(width, source.shape[1] - width)], low.at[at])]
                else:
                    parts = [
                        (source.at[:, pl.ds(0, tail_width)], normed.at[at, pl.ds(out_width, tail_width)]),
                        (source.at[:, pl.ds(tail_width, out_width)], delta.at[at]),
                        (source.at[:, pl.ds(width, source.shape[1] - width)], low_grad.at[at]),
                    ]
                copies += parts
                begin += size
        return copies

    def piece_copies(first_layer):
        copies = []
        begin = 0
        target = delta if first_layer else head
        mine = deltas if first_layer else heads
        own = delta_own if first_layer else head_own
        for side in (0, 1):
            start = half * (core if side == 0 else 1 - core)
            copies.append((own.at[pl.ds(pl.multiple_of(start, CHUNK), half)], target.at[pl.ds(begin, half)]))
            begin += half
            for source in mine if side == 0 else lates:
                copies.append((source, target.at[pl.ds(begin, source.shape[0])]))
                begin += source.shape[0]
        return copies

    def started(pairs):
        copies = [pltpu.make_async_copy(a, b, sems.at[i]) for i, (a, b) in enumerate(pairs)]
        for copy in copies:
            copy.start()
        return copies

    def masked(value, out):
        begin = 0
        for slot, size in zip(block_slots, piece * 2):
            at = slice(begin, begin + size)
            out[at, :] = jnp.where(slot_columns(slot, rank, out.shape[1]), value[at], 0.0).astype(bf16)
            begin += size

    @pl.when(core == 0)
    def _():
        copies = started(piece_copies(True) + batch_copies(True))
        for copy in copies[: 2 * len(piece)]:
            copy.wait()
        masked(product(delta[...], up[...], (1, 1)), low_grad)
        for copy in copies[2 * len(piece) :]:
            copy.wait()

    @pl.when(core != 0)
    def _():
        copies = started(piece_copies(False) + batch_copies(False))
        for copy in copies:
            copy.wait()

        def step(index, carry):
            at = pl.ds(pl.multiple_of(index * CHUNK, CHUNK), CHUNK)
            new, old = head[at, :].astype(f32), normed[at, out_width:].astype(f32)
            total = jnp.sum(new * new, axis=1, keepdims=True) + jnp.sum(old * old, axis=1, keepdims=True)
            inverse = lax.rsqrt(total / width + epsilon)
            normed[at, :out_width] = (new * inverse * gain_1[:, :out_width]).astype(bf16)
            normed[at, out_width:] = (old * inverse * gain_1[:, out_width:]).astype(bf16)
            return carry

        lax.fori_loop(0, rows // CHUNK, step, 0)
        masked(product(normed[...], down[...], (1, 1)), low)

    copies = []
    for left, right, out, target in ((low_grad, normed, out_down, grad_down), (low, delta, out_up, grad_up)):
        turned = left[...].T
        tile = 512
        for at in range(0, out.shape[1], tile):
            span = pl.ds(at, tile)
            out[:, span] = product(turned, right[:, span], (1, 0))
            copy = pltpu.make_async_copy(out.at[:, span], target.at[:, span], out_sems.at[len(copies)])
            copy.start()
            copies.append(copy)
    for copy in copies:
        copy.wait()


def ring_body(
    latents,
    out_grad,
    frozen_weight,
    norm_gain,
    time_gate,
    down_factors,
    up_factors,
    block_jobs,
    owners,
    block_steps,
    block_fill,
):
    f32, bf16 = jnp.float32, jnp.bfloat16
    core = lax.axis_index("section")
    member = lax.axis_index("dp")
    count = lax.axis_size("dp")
    rows, width = latents.shape
    half = rows // 2
    slots, rank = down_factors.shape[1:3]
    columns = slots * rank
    out_width = up_factors.shape[3]
    own_columns = frozen_weight.shape[1]
    first = core == 0
    place = ring_place(member, count)
    away = ring_pairs(lax.axis_size("groups"), count, 1)
    back = ring_pairs(lax.axis_size("groups"), count, -1)
    axes = ("groups", "dp", "section")
    outward = lambda value: lax.ppermute(value, axes, away)
    inward = lambda value: lax.ppermute(value, axes, back)
    reach = count // 2

    small = jnp.concatenate([norm_gain[0], time_gate[0]])
    small_in = swapped(small)
    small_0 = jnp.where(first, small, small_in)
    small_1 = jnp.where(first, small_in, small)
    gain_0, gain_1 = small_0[None, :width], small_1[None, :width]
    chosen = block_steps[0] == jnp.arange(time_gate.shape[1], dtype=jnp.int32)
    scale_0 = jnp.sum(jnp.where(chosen, small_0[width:], 0.0))
    scale_1 = jnp.sum(jnp.where(chosen, small_1[width:], 0.0))
    live = jnp.arange(rows, dtype=jnp.int32)[:, None] < block_fill[0]
    delta_1 = (scale_1 * jnp.where(live, out_grad[:, :out_width], 0.0)).astype(bf16)

    def halved(value):
        return lax.dynamic_slice(value, (core * half, 0), (half, value.shape[1]))

    def spread(value):
        arrived = []
        for hop in range(1, reach + 1):
            value = outward(halved(value) if hop == reach else value)
            arrived.append(value)
        return arrived

    lat_near, delta_near = spread(latents), spread(delta_1)

    down, up = down_factors[0].reshape(columns, width), up_factors[0].reshape(columns, out_width)
    frozen = frozen_weight[0]
    sources = [down, up, frozen, *map(swapped, (down, up, frozen))]

    matches = block_jobs[:, None] == jnp.arange(owners.shape[0], dtype=jnp.int32)[None, :]
    slot_of = jnp.sum(jnp.where(matches, owners[None, :], 0), axis=1) - member * slots
    steps = jnp.arange(reach + 1, dtype=jnp.int32)
    toward = jnp.where(first, -1, 1)
    blocks = ring_member(jnp.concatenate([place + toward * steps, place - toward * steps]), count)
    picked = blocks[:, None] == jnp.arange(count, dtype=jnp.int32)[None, :]
    block_slots = jnp.sum(jnp.where(picked, slot_of[None, :], 0), axis=1)

    def listed(*values):
        return jnp.stack([jnp.asarray(value, jnp.int32) for value in values])

    offset = member * own_columns
    gains = (gain_0, gain_1)

    def contributed(scalars, segments):
        return contribution(scalars, segments, gains, sources, slots, rank, out_width)

    head_scalars = listed(core, offset)
    all_scalars = jnp.concatenate([head_scalars, block_slots])
    near = [
        contributed(
            all_scalars,
            [(latents, delta_1, half), (lat_near[0], delta_near[0], rows)],
        )
    ]
    for hop in range(2, reach + 1):
        lat, delta = lat_near[hop - 1], delta_near[hop - 1]
        scalars = jnp.concatenate([head_scalars, block_slots[hop : hop + 1]])
        near.append(contributed(scalars, [(lat, delta, lat.shape[0])]))
    gots = [swapped(each[4]) for each in near]

    starts = [(0, half), *((half if hop == 1 else 0, rows) for hop in range(1, reach)), (0, half)]
    update_in = head_in = None
    for hop in range(reach, -1, -1):
        update, head, inner = near[max(hop - 1, 0)][:3]
        start, size = starts[hop]
        update_out = chained(head_scalars, update_in, update, start, size)
        head_out = chained(head_scalars, head_in, head, start, size, inner)
        pass_on = inward if hop else swapped
        update_in, head_in = pass_on(update_out), pass_on(head_out)
    head_next, delta_0 = call(
        owner_kernel,
        [shaped(bf16, rows, out_width)] * 2,
        [listed(core, block_fill[0]), scale_0[None], update_out, update_in, head_out, head_in, latents, out_grad[:, :out_width], gain_1],
        [pltpu.SMEM] * 2 + [pltpu.VMEM] * 7,
    )

    head_near, delta_0_near = spread(head_next), spread(delta_0)
    lates = [swapped(jnp.where(first, a, b)) for a, b in zip(head_near, delta_0_near)]

    sizes = [each[3].shape[0] for each in near]
    total = 2 * sum(sizes)
    args = [all_scalars, gain_1, *(each[3] for each in near), *gots, head_next, delta_0, *head_near, *delta_0_near, *lates, down, up]
    spaces = [pltpu.SMEM, pltpu.VMEM] + [pl.ANY] * (len(args) - 4) + [pltpu.VMEM] * 2
    grad_down, grad_up = call(
        lambda *refs: gradient_kernel(sizes, rank, *refs),
        [shaped(f32, columns, width), shaped(f32, columns, out_width)],
        args,
        spaces,
        [
            pltpu.VMEM((total, width), bf16),
            pltpu.VMEM((total, columns), bf16),
            pltpu.VMEM((total, columns), bf16),
            pltpu.VMEM((total, out_width), bf16),
            pltpu.VMEM((total, out_width), bf16),
            pltpu.VMEM((columns, width), f32),
            pltpu.VMEM((columns, out_width), f32),
            pltpu.SemaphoreType.DMA((2 * (reach + 1) + 6 * reach,)),
            pltpu.SemaphoreType.DMA(((width + out_width) // 512,)),
        ],
        flops=2 * total * columns * (width + 2 * out_width),
        out_spaces=[pl.ANY, pl.ANY],
    )
    return (
        grad_down.reshape(1, slots, rank, width),
        grad_up.reshape(1, slots, rank, out_width),
    )


def body(*arrays):
    latents, up_factors, block_fill = arrays[0], arrays[6], arrays[10]
    count = lax.axis_size("dp")
    rows, width = latents.shape
    out_width = up_factors.shape[3]
    own_columns = arrays[2].shape[1]
    gathered = count * rows * (2 * width + 4 * out_width) * 2
    fits = (
        block_fill.shape[0] == 1
        and count % 2 == 0
        and count >= 4
        and rows % 32 == 0
        and width % 512 == 0
        and out_width % 512 == 0
        and own_columns % 128 == 0
        and out_width % own_columns == 0
        and lax.axis_size("section") == 2
        and gathered <= 48 * 2**20
    )
    return ring_body(*arrays) if fits else spread_body(*arrays)


def solution(mesh):
    placed = (
        P(("groups", "dp"), None),
        P(("groups", "dp"), None),
        P("section", "dp", None),
        P("section", None),
        P("section", None),
        P("section", ("groups", "dp"), None, None),
        P("section", ("groups", "dp"), None, None),
        P("groups"),
        P("groups"),
        P(("groups", "dp")),
        P(("groups", "dp")),
    )
    return jax.shard_map(
        body,
        mesh=mesh,
        in_specs=placed,
        out_specs=(
            P("section", ("groups", "dp"), None, None),
            P("section", ("groups", "dp"), None, None),
        ),
        check_vma=False,
    )
```
